32 devices in a mesh: slab: 8 (over z, x), ang: 4 (over y, core).
Axes of the slice: x: 2, y: 2, z: 4, core: 2. Of those that a mesh axis runs over, the one named last changes fastest.
Arguments:
- volume: float32 [32, 128, 4096], P('slab', 'ang'), may hold values from -6 to 6
- measured: float32 [16, 512, 4096], P('ang', 'slab'), may hold values from -6 to 6
- incidence: int32 [16, 8, 5], P('ang', 'slab'), may hold values 0 or 1
- row_weights: float32 [16, 5, 4, 64], P('ang'), may hold values from -1.25 to 1.25
- path_table: float32 [2048, 128], P(None, 'ang'), may hold values from -0.5 to 0.5
- subset: int32 [16], replicated, may hold values from 0 to 2047
- gain_map: int32 [8, 64], P('slab'), may hold values from 0 to 4095
- gain_values: float32 [4096], replicated, may hold values from 0.5 to 1.5
Outputs:
- volume_next: float32 [32, 128, 4096], P('slab', 'ang')
- gain_next: float32 [4096], replicated
The draws below stay inside these ranges and needn't reach their ends.
All inputs are finite; a program needn't handle non-finite values. No bound on the sum of `incidence` on one device may be relied on, other than what follows from the above.
Results may differ from the reference program's by a relative error of at most 0.0003.
Values sent between devices are 32-bit elements; how exact they have to be, the bound alone decides.
A program may use at most 64 MiB of HBM per device.

```python
import jax
import jax.numpy as jnp
from jax import lax

DETECTOR_COLUMNS = 4096
GAIN_BLOCK_SIZE = 64
NG = 4096
NALL = 2048
ZD = 4
REACH = 2
SUBSET_ANGLES = 16
SLAB_COUNT = 8
NZ = 32
XV = 128
NR = 512
UB = 64


def touch_ends(result, own_key, least, high):
    extent = result.shape
    spot = [jax.random.randint(jax.random.fold_in(own_key, axis), (), 0, extent[axis]) for axis in range(len(extent))]
    result = result.at[tuple(spot)].set(least)
    longest = extent.index(max(extent))
    spot[longest] = (spot[longest] + 1) % extent[longest]
    return result.at[tuple(spot)].set(high)


def level_of(key, extent, shards, low, high):
    level, own = 1.0, jax.random.fold_in(key, 6)
    for position, parts in shards:
        heights = jnp.exp(jax.random.uniform(jax.random.fold_in(own, position), (parts,), jnp.float32, low / len(shards), high / len(shards)))
        level = level * jnp.repeat(heights, extent[position] // parts).reshape([-1 if axis == position else 1 for axis in range(len(extent))])
    return level


def bell_draw(key, dims, width, limit, split=(), kind=jnp.bfloat16):
    drawn = jax.random.normal(key, dims, jnp.float32) * width
    if len(split) > 0:
        drawn = level_of(key, dims, split, -0.22, 0.18) * drawn
    return jnp.clip(drawn, min=-limit, max=limit).astype(kind)


def setup_inputs(seed: int = 0) -> dict:
    seeds = jax.random.split(jax.random.key(seed), 9)
    volume = bell_draw(seeds[0], (NZ, XV, DETECTOR_COLUMNS), 1.0, 6.0, ((0, 8), (1, 4)), jnp.float32)
    measured = bell_draw(seeds[1], (SUBSET_ANGLES, NR, DETECTOR_COLUMNS), 1.0, 6.0, ((0, 4), (1, 8)), jnp.float32)
    incidence = touch_ends((jax.random.randint(seeds[2], (SUBSET_ANGLES, SLAB_COUNT, 2 * REACH + 1), 0, 4) < 3).astype(jnp.int32), jax.random.fold_in(seeds[2], 1), 0, 1)
    row_weights = bell_draw(seeds[3], (SUBSET_ANGLES, 2 * REACH + 1, ZD, GAIN_BLOCK_SIZE), (ZD * (2 * REACH + 1)) ** -0.5, 1.25, ((0, 4),), jnp.float32)
    path_table = bell_draw(seeds[4], (NALL, XV), XV ** -0.5, 0.5, ((1, 4),), jnp.float32)
    subset = touch_ends(jax.random.randint(seeds[5], (SUBSET_ANGLES,), 0, NALL), jax.random.fold_in(seeds[5], 1), 0, NALL - 1).astype(jnp.int32)
    gain_map = touch_ends(jax.random.randint(seeds[6], (SLAB_COUNT, UB), 0, NG), jax.random.fold_in(seeds[6], 1), 0, NG - 1).astype(jnp.int32)
    gain_values = jnp.clip(1.0 + 0.1 * jax.random.normal(seeds[7], (NG,), jnp.float32), 0.5, 1.5)
    return {"volume": volume, "measured": measured, "incidence": incidence, "row_weights": row_weights, "path_table": path_table, "subset": subset, "gain_map": gain_map, "gain_values": gain_values}


HIGH = lax.Precision.HIGHEST

def tv_from_padded(padded):
    lower = padded[:-1]
    diff_z = padded[1:] - lower
    diff_u = jnp.concatenate([lower[..., 1:], jnp.zeros_like(lower[..., :1])], axis=-1) - lower
    magnitude = jnp.sqrt(diff_z * diff_z + diff_u * diff_u + 0.25)
    flux_z = diff_z / magnitude
    flux_u = diff_u / magnitude
    moved_u = jnp.concatenate([jnp.zeros_like(flux_u[..., :1]), flux_u[..., :-1]], axis=-1)
    return flux_z[:-1] - flux_z[1:] + moved_u[1:] - flux_u[1:]

def reference(volume, measured, incidence, row_weights, path_table, subset, gain_map, gain_values):
    weights = path_table[subset]
    lines = jnp.einsum('ax,zxu->azu', weights, volume, precision=HIGH)
    lines = lines.reshape(SUBSET_ANGLES, SLAB_COUNT, ZD, DETECTOR_COLUMNS)
    padded = jnp.pad(lines, ((0, 0), (REACH, REACH), (0, 0), (0, 0)))
    forward_projection = jnp.zeros((SUBSET_ANGLES, SLAB_COUNT, GAIN_BLOCK_SIZE, DETECTOR_COLUMNS), jnp.float32)
    for offset in range(2 * REACH + 1):
        mask = incidence[:, :, offset].astype(jnp.float32)[:, :, None, None]
        forward_projection = forward_projection + mask * jnp.einsum('azr,abzu->abru', row_weights[:, offset], padded[:, offset:offset + SLAB_COUNT], precision=HIGH)
    measured_counts = measured.reshape(SUBSET_ANGLES, SLAB_COUNT, GAIN_BLOCK_SIZE, DETECTOR_COLUMNS)
    detector_pixel_gain = jnp.repeat(gain_values[gain_map], GAIN_BLOCK_SIZE, axis=1)[None, :, None, :]
    projection_residual = detector_pixel_gain * forward_projection - measured_counts
    weighted = detector_pixel_gain * projection_residual
    cross = (projection_residual * forward_projection).reshape(SUBSET_ANGLES, SLAB_COUNT, GAIN_BLOCK_SIZE, UB, GAIN_BLOCK_SIZE).sum(axis=(0, 2, 4))
    energy = (forward_projection * forward_projection).reshape(SUBSET_ANGLES, SLAB_COUNT, GAIN_BLOCK_SIZE, UB, GAIN_BLOCK_SIZE).sum(axis=(0, 2, 4))
    cross_sum = jax.ops.segment_sum(cross.reshape(-1), gain_map.reshape(-1), num_segments=NG)
    energy_sum = jax.ops.segment_sum(energy.reshape(-1), gain_map.reshape(-1), num_segments=NG)
    gain_next = gain_values - cross_sum / (energy_sum + 1.0)
    grads = jnp.zeros((SUBSET_ANGLES, SLAB_COUNT + 2 * REACH, ZD, DETECTOR_COLUMNS), jnp.float32)
    for offset in range(2 * REACH + 1):
        mask = incidence[:, :, offset].astype(jnp.float32)[:, :, None, None]
        part = jnp.einsum('azr,abru->abzu', row_weights[:, offset], weighted, precision=HIGH) * mask
        grads = grads.at[:, offset:offset + SLAB_COUNT].add(part)
    images = grads[:, REACH:REACH + SLAB_COUNT].reshape(SUBSET_ANGLES, NZ, DETECTOR_COLUMNS)
    gradient = jnp.einsum('ax,azu->zxu', weights, images, precision=HIGH)
    smooth = tv_from_padded(jnp.pad(volume, ((1, 1), (0, 0), (0, 0))))
    volume_next = volume - 0.2 * gradient - 0.2 * smooth
    return (volume_next, gain_next)
```

```python
import functools

import jax
import jax.numpy as jnp
from jax import lax
from jax.experimental import pallas as pl
from jax.experimental.pallas import tpu as pltpu
from jax.sharding import PartitionSpec as P

F32 = jnp.float32
BF16 = jnp.bfloat16
MESH = pl.DeviceIdType.MESH
CHUNKS = 4
LAGS = (0, 1, 2, 3, 4, 5, 6, 7, 8)
HALO_STEPS = (0, 0, 4, 6)
TV_STEPS = (5, 6, 7, 8)
KINDS = 11
A, B, FQ, FP, FM, FR, BD, BS, BP, GY, GC = range(KINDS)


def split2(x):
    hi = x.astype(BF16)
    return hi, (x - hi.astype(F32)).astype(BF16)


def split3(x):
    hi = x.astype(BF16).astype(F32)
    mid = (x - hi).astype(BF16).astype(F32)
    return hi, mid, x - hi - mid


def dot(a, b):
    return jnp.dot(a, b, preferred_element_type=F32)


def dot_nt(a, b):
    return lax.dot_general(a, b, (((1,), (1,)), ((), ())), preferred_element_type=F32)


def kernel(
    n, na, planes, xd, al, block,
    inc, subset, vol_hbm, meas_hbm, rw, pt, gmap, gv,
    out_hbm, gain_out,
    vol, meas, base, halo, wf, wst, wt, bf, bst, bt,
    part, ra, acc, rb, lin, cb, rd, rs, pb, rp, img, outv,
    gt, pg, st, gm, ga, gr, gs,
    vol_sem, meas_sem, out_sem, send_sem, recv_sem,
    hs_sem, hr_sem, ks_sem, kr_sem, ss_sem, sr_sem,
):
    cols = vol.shape[1]
    width = cols // CHUNKS
    groups = na // 2
    taps = rw.shape[1]
    lr = al * planes
    s = lax.axis_index("slab")
    ang = lax.axis_index("ang")
    core = lax.rem(ang, 2)
    y = ang // 2
    par = lax.rem(s, 2)
    sgn = 1 - 2 * par
    q = s + sgn
    fwd_to = s + 2 * sgn
    fwd_from = s - 2 * sgn
    fwd_ok = jnp.logical_and(fwd_to >= 0, fwd_to < n)
    back_ok = jnp.logical_and(fwd_from >= 0, fwd_from < n)
    up_ok = s + 2 < n
    dn_ok = s >= 2
    pieces = halo.shape[1]
    prow = halo.shape[2]

    def span(c):
        return pl.ds(c * width, width)

    vol_copies = [
        pltpu.make_async_copy(vol_hbm.at[:, span(c)], vol.at[:, span(c)], vol_sem.at[c])
        for c in range(CHUNKS)
    ]
    meas_copies = [
        pltpu.make_async_copy(meas_hbm.at[:, span(c)], meas.at[:, span(c)], meas_sem.at[c])
        for c in range(CHUNKS)
    ]
    for copy in vol_copies + meas_copies:
        copy.start()

    barrier = pltpu.get_barrier_semaphore()
    for i in range(1, na):
        pl.semaphore_signal(barrier, inc=1, device_id=(s, lax.rem(ang + i, na)), device_id_type=MESH)

    @pl.loop(1, n)
    def _(i):
        pl.semaphore_signal(barrier, inc=1, device_id=(lax.rem(s + i, n), ang), device_id_type=MESH)

    wf[...] = jnp.zeros_like(wf)
    for c in range(2):
        for g in range(groups):
            for a in range(al):
                line = pt[pl.ds(subset[(g * 2 + c) * al + a], 1), :]
                for z in range(planes):
                    row = ((c * groups + g) * al + a) * planes + z
                    wf[row : row + 1, z * xd : (z + 1) * xd] = line
    w = wf[...]
    whi, wlo = split2(w)
    wst[...] = jnp.concatenate([whi, wlo], axis=0)

    pl.semaphore_wait(barrier, na - 1 + n - 1)

    def remote(src, dst, kind, c, slab, a):
        return pltpu.make_async_remote_copy(
            src_ref=src, dst_ref=dst, send_sem=send_sem.at[kind, c], recv_sem=recv_sem.at[kind, c],
            device_id=(slab, a), device_id_type=MESH,
        )

    other = y * 2 + 1 - core

    def make(kind, c):
        u = span(c)
        if kind == A:
            return remote(part.at[1 - core, :, u], ra.at[:, u], A, c, s, other)
        if kind == B:
            return remote(acc.at[1 - y, :, u], rb.at[:, u], B, c, s, (1 - y) * 2 + core)
        if kind == FQ:
            return remote(lin.at[2, :, u], lin.at[1 + 2 * par, :, u], FQ, c, q, ang)
        if kind == FP:
            return remote(lin.at[2, :, u], lin.at[0, :, u], FP, c, s + 2, ang)
        if kind == FM:
            return remote(lin.at[2, :, u], lin.at[4, :, u], FM, c, s - 2, ang)
        if kind == FR:
            return remote(lin.at[3 - 2 * par, :, u], lin.at[1 + 2 * par, :, u], FR, c, fwd_to, ang)
        if kind == BD:
            return remote(cb.at[pl.ds(3 * par, 2), :, u], rd.at[:, :, u], BD, c, fwd_from, ang)
        if kind == BS:
            return remote(cb.at[4 * (1 - par), :, u], rs.at[:, u], BS, c, fwd_to, ang)
        if kind == BP:
            return remote(pb.at[:, u], rp.at[:, u], BP, c, q, ang)
        if kind == GY:
            return remote(img.at[core, y, :, u], img.at[core, y, :, u], GY, c, s, (1 - y) * 2 + core)
        return remote(img.at[core, :, :, u], img.at[core, :, :, u], GC, c, s, other)

    sends = {FP: up_ok, FM: dn_ok, FR: fwd_ok, BD: back_ok, BS: fwd_ok}
    arrives = {FP: dn_ok, FM: up_ok, FR: back_ok, BD: fwd_ok, BS: back_ok}

    def guarded(table, kind, run):
        if kind in table:
            pl.when(table[kind])(run)
        else:
            run()

    def start(kind, c):
        guarded(sends, kind, lambda: make(kind, c).start())

    def arrive(kind, c):
        guarded(arrives, kind, lambda: make(kind, c).wait_recv())

    def halo_copy(side, i):
        rows = pl.ds((planes - 1) * xd + i * prow if side == 0 else i * prow, prow)
        return pltpu.make_async_remote_copy(
            src_ref=vol_hbm.at[rows, :], dst_ref=halo.at[side, i],
            send_sem=hs_sem.at[side, i], recv_sem=hr_sem.at[side, i],
            device_id=(s + 1 if side == 0 else s - 1, ang), device_id_type=MESH,
        )

    low_ok = s >= 1
    high_ok = s + 1 < n

    def halo_start(i):
        pl.when(high_ok)(lambda: halo_copy(0, i).start())
        pl.when(low_ok)(lambda: halo_copy(1, i).start())

    def zero(ref, when):
        @pl.when(when)
        def _():
            ref[...] = jnp.zeros(ref.shape, ref.dtype)

    def prepare():
        zero(lin.at[0], jnp.logical_not(dn_ok))
        zero(lin.at[4], jnp.logical_not(up_ok))
        zero(lin.at[1 + 2 * par], jnp.logical_not(back_ok))
        zero(rd, jnp.logical_not(fwd_ok))
        zero(rs, jnp.logical_not(back_ok))
        zero(halo.at[0], jnp.logical_not(low_ok))
        zero(halo.at[1], jnp.logical_not(high_ok))
        hi32 = whi.astype(F32)
        pad = jnp.zeros((wt.shape[1] - 3 * w.shape[0], w.shape[1]), F32)
        wt[...] = jnp.concatenate([hi32, hi32, wlo.astype(F32), pad], axis=0).T.astype(BF16)
        bf[...] = jnp.zeros_like(bf)
        for a in range(al):
            for k in range(taps):
                mask = inc[a, 0, k].astype(F32)
                row = (k * al + a) * planes
                bf[row : row + planes, a * block : (a + 1) * block] = rw[a, k] * mask
        b = bf[...]
        bhi, blo = split2(b)
        bst[...] = jnp.concatenate([bhi, blo], axis=0)
        hi32 = bhi.astype(F32)
        pad = jnp.zeros((bt.shape[1] - 3 * b.shape[0], b.shape[1]), F32)
        bt[...] = jnp.concatenate([hi32, hi32, blo.astype(F32), pad], axis=0).T.astype(BF16)

    def prepare_gain():
        nb = gmap.shape[1]
        gm[...] = jnp.zeros_like(gm)
        g = gmap[...]
        hi = lax.shift_right_logical(g, 7)
        gm[2:3, 0:nb] = hi.astype(F32)
        gm[3:4, 0:nb] = (g - hi * 128).astype(F32)
        for c in range(CHUNKS):
            row = lax.broadcasted_iota(jnp.int32, (128, width), 0) * block
            col = lax.broadcasted_iota(jnp.int32, (128, width), 1) + c * width
            inside = jnp.logical_and(col >= row, col < row + block)
            gt[:, span(c)] = jnp.where(inside, 1.0, 0.0).astype(BF16)
        hi_row = gm[2:3, :]
        lo_row = gm[3:4, :]
        nh = gv.shape[0]
        lo_hot = jnp.where(
            lax.broadcasted_iota(jnp.int32, (128, 128), 0).astype(F32) == lo_row, 1.0, 0.0
        ).astype(BF16)
        hi_hot = lax.broadcasted_iota(jnp.int32, (nh, 128), 0).astype(F32) == hi_row
        parts = jnp.concatenate(split3(gv[...]), axis=0).astype(BF16)
        picked = dot(parts, lo_hot)
        picked = picked[:nh] + picked[nh : 2 * nh] + picked[2 * nh : 3 * nh]
        gain = jnp.sum(jnp.where(hi_hot, picked, 0.0), axis=0, keepdims=True)
        gain = jnp.broadcast_to(gain, (8, 128))
        zero8 = jnp.zeros((8, 128), F32)
        parts = jnp.concatenate([*split3(gain), zero8], axis=0).astype(BF16)
        for c in range(CHUNKS):
            wide = dot(parts, gt[:, span(c)])
            pg[:, span(c)] = wide[0:8] + wide[8:16] + wide[16:24]
        st[...] = jnp.zeros_like(st)

    def tv_piece(i):
        pl.when(low_ok)(lambda: halo_copy(0, i).wait_recv())
        pl.when(high_ok)(lambda: halo_copy(1, i).wait_recv())
        for c in range(CHUNKS):
            left = 0 if c == 0 else 128
            right = 0 if c == CHUNKS - 1 else 128
            begin = c * width - left
            full = width + left + right
            lane = lax.broadcasted_iota(jnp.int32, (prow, full), 1)

            def plane(z):
                if z < 0:
                    return halo[0, i, :, begin : begin + full]
                if z == planes:
                    return halo[1, i, :, begin : begin + full]
                r = z * xd + i * prow
                return vol[r : r + prow, begin : begin + full]

            here = plane(-1)
            before = None
            for z in range(-1, planes):
                above = plane(z + 1)
                dz = above - here
                shifted = pltpu.roll(here, full - 1, 1)
                if right == 0:
                    shifted = jnp.where(lane == full - 1, 0.0, shifted)
                du = shifted - here
                inv = lax.rsqrt(dz * dz + du * du + 0.25)
                fz = dz * inv
                if z >= 0:
                    fu = du * inv
                    moved = pltpu.roll(fu, 1, 1)
                    if left == 0:
                        moved = jnp.where(lane == 0, 0.0, moved)
                    smooth = before - fz + moved - fu
                    r = z * xd + i * prow
                    new = here - 0.2 * smooth
                    base[r : r + prow, c * width : (c + 1) * width] = new[:, left : left + width]
                before = fz
                here = above

    sub = min(256, width)

    def tiles(c, body):
        @pl.loop(0, width // sub)
        def _(t):
            body(pl.ds(pl.multiple_of(c * width + t * sub, sub), sub))

    wrows = w.shape[0]
    half = groups * lr

    def stage0(c):
        vol_copies[c].wait()

        def body(u):
            vhi, vlo = split2(vol[:, u])
            first = dot(wst[...], vhi)
            lines = first[:wrows] + first[wrows:] + dot(wst[0:wrows, :], vlo)
            part[0, :, u] = lines[:half]
            part[1, :, u] = lines[half:]

        tiles(c, body)
        start(A, c)

    def stage1(c):
        arrive(A, c)
        u = span(c)
        total = part[core, :, u] + ra[:, u]
        for g in range(groups):
            acc[g, :, u] = total[g * lr : (g + 1) * lr]
        start(B, c)

    def stage2(c):
        arrive(B, c)
        u = span(c)
        lin[2, :, u] = acc[y, :, u] + rb[:, u]
        start(FQ, c)
        start(FP, c)
        start(FM, c)

    def stage3(c):
        arrive(FQ, c)
        start(FR, c)

    brows = taps * lr

    def stage4(c):
        arrive(FP, c)
        arrive(FM, c)
        arrive(FR, c)
        meas_copies[c].wait()

        def body(u):
            lhi, llo = split2(lin[:, :, u].reshape(brows, sub))
            parts = [lhi, llo, lhi]
            if bt.shape[1] > 3 * brows:
                parts.append(jnp.zeros((bt.shape[1] - 3 * brows, sub), BF16))
            proj = dot(bt[...], jnp.concatenate(parts, axis=0))
            gain = pg[0:1, u]
            residual = gain * proj - meas[:, u]
            weighted = gain * residual
            st[0:1, u] = jnp.sum(residual * proj, axis=0, keepdims=True)
            st[1:2, u] = jnp.sum(proj * proj, axis=0, keepdims=True)
            hi, lo = split2(weighted)
            first = dot(bst[...], hi)
            terms = first[:brows] + first[brows:] + dot(bst[0:brows, :], lo)
            cb[:, :, u] = terms.reshape(taps, lr, sub)

        tiles(c, body)
        start(BD, c)
        start(BS, c)

    def stage5(c):
        arrive(BD, c)
        u = span(c)
        pb[:, u] = cb[3 - 2 * par, :, u] + rd[1 - par, :, u]
        start(BP, c)

    def stage6(c):
        arrive(BS, c)
        arrive(BP, c)
        u = span(c)
        img[core, y, :, u] = cb[2, :, u] + rd[par, :, u] + rs[:, u] + rp[:, u]
        start(GY, c)

    def gather_in(c):
        u = span(c)
        pltpu.make_async_remote_copy(
            src_ref=img.at[core, y, :, u], dst_ref=img.at[core, 1 - y, :, u],
            send_sem=send_sem.at[GY, c], recv_sem=recv_sem.at[GY, c],
            device_id=(s, (1 - y) * 2 + core), device_id_type=MESH,
        ).wait_recv()

    def stage7(c):
        gather_in(c)
        start(GC, c)

    def out_copy(c):
        return pltpu.make_async_copy(outv.at[:, span(c)], out_hbm.at[:, span(c)], out_sem.at[c])

    def stage8(c):
        u = span(c)
        pltpu.make_async_remote_copy(
            src_ref=img.at[core, :, :, u], dst_ref=img.at[1 - core, :, :, u],
            send_sem=send_sem.at[GC, c], recv_sem=recv_sem.at[GC, c],
            device_id=(s, other), device_id_type=MESH,
        ).wait_recv()

        def body(u):
            ihi, ilo = split2(img[:, :, :, u].reshape(wrows, sub))
            parts = [ihi, ilo, ihi]
            if wt.shape[1] > 3 * wrows:
                parts.append(jnp.zeros((wt.shape[1] - 3 * wrows, sub), BF16))
            gradient = dot(wt[...], jnp.concatenate(parts, axis=0))
            outv[:, u] = base[:, u] - 0.2 * gradient

        tiles(c, body)
        out_copy(c).start()

    def gain_peer(i):
        return pltpu.make_async_remote_copy(
            src_ref=ga, dst_ref=gr.at[i - 1], send_sem=ks_sem.at[i - 1], recv_sem=kr_sem.at[i - 1],
            device_id=(s, lax.rem(ang + i, na)), device_id_type=MESH,
        )

    def gain_first():
        rows = jnp.concatenate([*split3(st[...]), jnp.zeros(st.shape, F32)], axis=0).astype(BF16)
        sums = dot_nt(rows, gt[...])
        sums = sums[0:8] + sums[8:16] + sums[16:24]
        lane_row = lax.broadcasted_iota(jnp.int32, (8, 128), 0)
        ga[...] = jnp.where(lane_row < 2, sums, gm[...])
        for i in range(1, na):
            gain_peer(i).start()

    def gain_slab(i, slot):
        return pltpu.make_async_remote_copy(
            src_ref=gs.at[slot], dst_ref=gs.at[slot], send_sem=ss_sem.at[i], recv_sem=sr_sem.at[slot],
            device_id=(lax.rem(s + i, n), ang), device_id_type=MESH,
        )

    def gain_second():
        total = ga[...]
        for i in range(1, na):
            gain_peer(i).wait_recv()
            total = total + gr[i - 1]
        lane_row = lax.broadcasted_iota(jnp.int32, (8, 128), 0)
        gs[s] = jnp.where(lane_row < 2, total, gm[...])

        @pl.loop(1, n)
        def _(i):
            gain_slab(i, s).start()

    def gain_last():
        @pl.loop(1, n)
        def _(i):
            gain_slab(i, lax.rem(s + i, n)).wait_recv()

        nh = gv.shape[0]

        def body(i, total):
            m = gs[i]
            lo_hot = jnp.where(
                lax.broadcasted_iota(jnp.int32, (128, 128), 0).astype(F32) == m[3:4], 1.0, 0.0
            ).astype(BF16)
            hi_hot = lax.broadcasted_iota(jnp.int32, (nh, 128), 0).astype(F32) == m[2:3]
            rows = [
                jnp.where(hi_hot, x, 0.0) for k in range(2) for x in split3(m[k : k + 1])
            ]
            return total + dot_nt(jnp.concatenate(rows, axis=0).astype(BF16), lo_hot)

        total = lax.fori_loop(0, n, body, jnp.zeros((6 * nh, 128), F32))
        cross = total[:nh] + total[nh : 2 * nh] + total[2 * nh : 3 * nh]
        energy = total[3 * nh : 4 * nh] + total[4 * nh : 5 * nh] + total[5 * nh :]
        gain_out[...] = gv[...] - cross / (energy + 1.0)

    stages = (stage0, stage1, stage2, stage3, stage4, stage5, stage6, stage7, stage8)
    last_fwd = LAGS[4] + CHUNKS - 1
    for t in range(LAGS[8] + CHUNKS):
        for i in range(pieces):
            if HALO_STEPS[i] == t:
                halo_start(i)
        for i in range(pieces):
            if TV_STEPS[i] == t:
                tv_piece(i)
        if t == last_fwd + 3:
            gain_last()
        for k, stage in enumerate(stages):
            if 0 <= t - LAGS[k] < CHUNKS:
                stage(t - LAGS[k])
        if t == 0:
            prepare()
        if t == 1:
            prepare_gain()
        if t == last_fwd:
            gain_first()
        if t == last_fwd + 1:
            gain_second()

    for c in range(CHUNKS):
        for kind in range(KINDS):
            guarded(sends, kind, lambda: make(kind, c).wait_send())
    for i in range(pieces):
        pl.when(high_ok)(lambda: halo_copy(0, i).wait_send())
        pl.when(low_ok)(lambda: halo_copy(1, i).wait_send())
    for i in range(1, na):
        gain_peer(i).wait_send()

    @pl.loop(1, n)
    def _(i):
        gain_slab(i, s).wait_send()

    for c in range(CHUNKS):
        out_copy(c).wait()


def local(n, na, volume, measured, incidence, row_weights, path_table, subset, gain_map, gain_values):
    planes, xd, cols = volume.shape
    al, block, _ = measured.shape
    taps = row_weights.shape[1]
    params = gain_values.shape[0]
    groups = na // 2
    assert taps == 5 and n % 2 == 0 and na == 4 and params % 128 == 0 and cols // block <= 128
    lr = al * planes
    kv = planes * xd
    wrows = na * lr
    brows = taps * lr
    pieces = len(HALO_STEPS)
    up = lambda v: -(-v // 128) * 128
    vm = pltpu.VMEM
    dma = pltpu.SemaphoreType.DMA
    scratch = [
        vm((kv, cols), F32), vm((al * block, cols), F32), vm((kv, cols), F32),
        vm((2, pieces, xd // pieces, cols), F32),
        vm((wrows, kv), F32), vm((2 * wrows, kv), BF16), vm((kv, up(3 * wrows)), BF16),
        vm((brows, al * block), F32), vm((2 * brows, al * block), BF16),
        vm((al * block, up(3 * brows)), BF16),
        vm((2, groups * lr, cols), F32), vm((groups * lr, cols), F32), vm((groups, lr, cols), F32),
        vm((lr, cols), F32),
        vm((taps, lr, cols), F32), vm((taps, lr, cols), F32), vm((2, lr, cols), F32),
        vm((lr, cols), F32), vm((lr, cols), F32), vm((lr, cols), F32),
        vm((2, groups, lr, cols), F32), vm((kv, cols), F32),
        vm((128, cols), BF16), vm((8, cols), F32), vm((8, cols), F32),
        vm((8, 128), F32), vm((8, 128), F32), vm((na - 1, 8, 128), F32), vm((n, 8, 128), F32),
        dma((CHUNKS,)), dma((CHUNKS,)), dma((CHUNKS,)), dma((KINDS, CHUNKS)), dma((KINDS, CHUNKS)),
        dma((2, pieces)), dma((2, pieces)), dma((na - 1,)), dma((na - 1,)), dma((n,)), dma((n,)),
    ]
    smem = pl.BlockSpec(memory_space=pltpu.SMEM)
    vmem = pl.BlockSpec(memory_space=pltpu.VMEM)
    hbm = pl.BlockSpec(memory_space=pl.ANY)
    out, gain = pl.pallas_call(
        functools.partial(kernel, n, na, planes, xd, al, block),
        out_shape=(
            jax.ShapeDtypeStruct((kv, cols), F32),
            jax.ShapeDtypeStruct((params // 128, 128), F32),
        ),
        in_specs=[smem, smem, hbm, hbm, vmem, vmem, vmem, vmem],
        out_specs=(hbm, vmem),
        scratch_shapes=scratch,
        compiler_params=pltpu.CompilerParams(
            collective_id=0, has_side_effects=True, vmem_limit_bytes=56 * 1024 * 1024
        ),
        name="step",
    )(
        incidence, subset, volume.reshape(kv, cols), measured.reshape(al * block, cols),
        row_weights, path_table, gain_map, gain_values.reshape(params // 128, 128),
    )
    return out.reshape(planes, xd, cols), gain.reshape(params)


def solution(mesh):
    in_specs = (
        P("slab", "ang", None),
        P("ang", "slab", None),
        P("ang", "slab", None),
        P("ang", None, None, None),
        P(None, "ang"),
        P(),
        P("slab", None),
        P(),
    )
    out_specs = (P("slab", "ang", None), P())
    body = functools.partial(local, mesh.shape["slab"], mesh.shape["ang"])
    return jax.shard_map(body, mesh=mesh, in_specs=in_specs, out_specs=out_specs, check_vma=False)
```

```python
import functools

import jax
import jax.numpy as jnp
from jax import lax
from jax.experimental import pallas as pl
from jax.experimental.pallas import tpu as pltpu
from jax.sharding import PartitionSpec as P

F32 = jnp.float32
BF16 = jnp.bfloat16
MESH = pl.DeviceIdType.MESH
CHUNKS = 4
LAGS = (0, 1.5, 4.2, 7, 10, 14, 17, 20, 21.5)
PERIODS = (0.8, 1.5, 2, 2.5, 2.5, 2.5, 2.5, 2.5, 2.5)
ROW_PIECES = 4
HALO_FROM = -1.0
HALO_EARLY = 3
HALO_NEXT = 4.3
HALO_EVERY = 1.2
TV_AFTER = 4.0
PREP_AT = (0.4, 1.6)
GAIN_AFTER = (0.5, 3.5, 7.5)
KINDS = 11
A, B, FQ, FP, FM, FR, BD, BS, BP, GY, GC = range(KINDS)


def split2(x):
    hi = x.astype(BF16)
    return hi, (x - hi.astype(F32)).astype(BF16)


def split3(x):
    hi = x.astype(BF16).astype(F32)
    mid = (x - hi).astype(BF16).astype(F32)
    return hi, mid, x - hi - mid


def dot(a, b):
    return jnp.dot(a, b, preferred_element_type=F32)


def dot_nt(a, b):
    return lax.dot_general(a, b, (((1,), (1,)), ((), ())), preferred_element_type=F32)


def kernel(
    n, na, planes, xd, al, block,
    inc, subset, vol_hbm, meas_hbm, rw, pt, gmap, gv,
    outv, gain_out,
    vol, meas, base, halo, wf, wst, wt, bf, bst, bt,
    part, ra, acc, rb, lin, cb, rd, rs, pb, rp, img,
    gt, pg, st, gm, ga, gr, gs, pick,
    vol_sem, meas_sem, send_sem, recv_sem,
    hs_sem, hr_sem, ks_sem, kr_sem, ss_sem, sr_sem,
):
    cols = vol.shape[1]
    width = cols // CHUNKS
    groups = na // 2
    taps = rw.shape[1]
    lr = al * planes
    s = lax.axis_index("slab")
    ang = lax.axis_index("ang")
    core = lax.rem(ang, 2)
    y = ang // 2
    par = lax.rem(s, 2)
    sgn = 1 - 2 * par
    q = s + sgn
    fwd_to = s + 2 * sgn
    fwd_from = s - 2 * sgn
    fwd_ok = jnp.logical_and(fwd_to >= 0, fwd_to < n)
    back_ok = jnp.logical_and(fwd_from >= 0, fwd_from < n)
    up_ok = s + 2 < n
    dn_ok = s >= 2
    rows_split = ROW_PIECES
    prow = xd // rows_split
    pieces = rows_split * CHUNKS

    def span(c):
        return pl.ds(c * width, width)

    vol_copies = [
        pltpu.make_async_copy(vol_hbm.at[:, span(c)], vol.at[:, span(c)], vol_sem.at[c])
        for c in range(CHUNKS)
    ]
    meas_copies = [
        pltpu.make_async_copy(meas_hbm.at[:, span(c)], meas.at[:, span(c)], meas_sem.at[c])
        for c in range(CHUNKS)
    ]
    for copy in vol_copies + meas_copies:
        copy.start()

    barrier = pltpu.get_barrier_semaphore()
    for i in range(1, na):
        pl.semaphore_signal(barrier, inc=1, device_id=(s, lax.rem(ang + i, na)), device_id_type=MESH)

    @pl.loop(1, n)
    def _(i):
        pl.semaphore_signal(barrier, inc=1, device_id=(lax.rem(s + i, n), ang), device_id_type=MESH)

    count = pick.shape[0]
    rows_all = pick.shape[1]
    spot = lax.broadcasted_iota(jnp.int32, (1, rows_all), 1)
    for a in range(count):
        pick[a : a + 1, :] = jnp.where(spot == subset[a], 1.0, 0.0)
    table = jnp.concatenate(split3(pt[...]), axis=0).astype(BF16)
    chosen = dot_nt(pick[...].astype(BF16), table)
    chosen = chosen[:, :xd] + chosen[:, xd : 2 * xd] + chosen[:, 2 * xd : 3 * xd]
    wf[...] = jnp.zeros_like(wf)
    for c in range(2):
        for g in range(groups):
            for a in range(al):
                angle = (g * 2 + c) * al + a
                line = chosen[angle : angle + 1, :]
                for z in range(planes):
                    row = ((c * groups + g) * al + a) * planes + z
                    wf[row : row + 1, z * xd : (z + 1) * xd] = line
    w = wf[...]
    whi, wlo = split2(w)
    wst[...] = jnp.concatenate([whi, wlo], axis=0)

    pl.semaphore_wait(barrier, na - 1 + n - 1)

    def remote(src, dst, kind, c, slab, a):
        return pltpu.make_async_remote_copy(
            src_ref=src, dst_ref=dst, send_sem=send_sem.at[kind, c], recv_sem=recv_sem.at[kind, c],
            device_id=(slab, a), device_id_type=MESH,
        )

    other = y * 2 + 1 - core

    def make(kind, c):
        u = span(c)
        if kind == A:
            return remote(part.at[1 - core, :, u], ra.at[:, u], A, c, s, other)
        if kind == B:
            return remote(acc.at[1 - y, :, u], rb.at[:, u], B, c, s, (1 - y) * 2 + core)
        if kind == FQ:
            return remote(lin.at[2, :, u], lin.at[1 + 2 * par, :, u], FQ, c, q, ang)
        if kind == FP:
            return remote(lin.at[2, :, u], lin.at[0, :, u], FP, c, s + 2, ang)
        if kind == FM:
            return remote(lin.at[2, :, u], lin.at[4, :, u], FM, c, s - 2, ang)
        if kind == FR:
            return remote(lin.at[3 - 2 * par, :, u], lin.at[1 + 2 * par, :, u], FR, c, fwd_to, ang)
        if kind == BD:
            return remote(cb.at[pl.ds(3 * par, 2), :, u], rd.at[:, :, u], BD, c, fwd_from, ang)
        if kind == BS:
            return remote(cb.at[4 * (1 - par), :, u], rs.at[:, u], BS, c, fwd_to, ang)
        if kind == BP:
            return remote(pb.at[:, u], rp.at[:, u], BP, c, q, ang)
        if kind == GY:
            return remote(img.at[core, y, :, u], img.at[core, y, :, u], GY, c, s, (1 - y) * 2 + core)
        return remote(img.at[core, :, :, u], img.at[core, :, :, u], GC, c, s, other)

    sends = {FP: up_ok, FM: dn_ok, FR: fwd_ok, BD: back_ok, BS: fwd_ok}
    arrives = {FP: dn_ok, FM: up_ok, FR: back_ok, BD: fwd_ok, BS: back_ok}

    def guarded(table, kind, run):
        if kind in table:
            pl.when(table[kind])(run)
        else:
            run()

    def start(kind, c):
        guarded(sends, kind, lambda: make(kind, c).start())

    def arrive(kind, c):
        guarded(arrives, kind, lambda: make(kind, c).wait_recv())

    def halo_copy(side, i):
        r, c = i // CHUNKS, i % CHUNKS
        rows = pl.ds((planes - 1) * xd + r * prow if side == 0 else r * prow, prow)
        return pltpu.make_async_remote_copy(
            src_ref=vol_hbm.at[rows, span(c)], dst_ref=halo.at[side, pl.ds(r * prow, prow), span(c)],
            send_sem=hs_sem.at[side, i], recv_sem=hr_sem.at[side, i],
            device_id=(s + 1 if side == 0 else s - 1, ang), device_id_type=MESH,
        )

    low_ok = s >= 1
    high_ok = s + 1 < n

    def halo_start(i):
        pl.when(high_ok)(lambda: halo_copy(0, i).start())
        pl.when(low_ok)(lambda: halo_copy(1, i).start())

    def zero(ref, when):
        @pl.when(when)
        def _():
            ref[...] = jnp.zeros(ref.shape, ref.dtype)

    def prepare():
        zero(lin.at[0], jnp.logical_not(dn_ok))
        zero(lin.at[4], jnp.logical_not(up_ok))
        zero(lin.at[1 + 2 * par], jnp.logical_not(back_ok))
        zero(rd, jnp.logical_not(fwd_ok))
        zero(rs, jnp.logical_not(back_ok))
        zero(halo.at[0], jnp.logical_not(low_ok))
        zero(halo.at[1], jnp.logical_not(high_ok))
        hi32 = whi.astype(F32)
        pad = jnp.zeros((wt.shape[1] - 3 * w.shape[0], w.shape[1]), F32)
        wt[...] = jnp.concatenate([hi32, hi32, wlo.astype(F32), pad], axis=0).T.astype(BF16)
        bf[...] = jnp.zeros_like(bf)
        for a in range(al):
            for k in range(taps):
                mask = inc[a, 0, k].astype(F32)
                row = (k * al + a) * planes
                bf[row : row + planes, a * block : (a + 1) * block] = rw[a, k] * mask
        b = bf[...]
        bhi, blo = split2(b)
        bst[...] = jnp.concatenate([bhi, blo], axis=0)
        hi32 = bhi.astype(F32)
        pad = jnp.zeros((bt.shape[1] - 3 * b.shape[0], b.shape[1]), F32)
        bt[...] = jnp.concatenate([hi32, hi32, blo.astype(F32), pad], axis=0).T.astype(BF16)

    def prepare_gain():
        nb = gmap.shape[1]
        gm[...] = jnp.zeros_like(gm)
        g = gmap[...]
        hi = lax.shift_right_logical(g, 7)
        gm[2:3, 0:nb] = hi.astype(F32)
        gm[3:4, 0:nb] = (g - hi * 128).astype(F32)
        for c in range(CHUNKS):
            row = lax.broadcasted_iota(jnp.int32, (128, width), 0) * block
            col = lax.broadcasted_iota(jnp.int32, (128, width), 1) + c * width
            inside = jnp.logical_and(col >= row, col < row + block)
            gt[:, span(c)] = jnp.where(inside, 1.0, 0.0).astype(BF16)
        hi_row = gm[2:3, :]
        lo_row = gm[3:4, :]
        nh = gv.shape[0]
        lo_hot = jnp.where(
            lax.broadcasted_iota(jnp.int32, (128, 128), 0).astype(F32) == lo_row, 1.0, 0.0
        ).astype(BF16)
        hi_hot = lax.broadcasted_iota(jnp.int32, (nh, 128), 0).astype(F32) == hi_row
        parts = jnp.concatenate(split3(gv[...]), axis=0).astype(BF16)
        picked = dot(parts, lo_hot)
        picked = picked[:nh] + picked[nh : 2 * nh] + picked[2 * nh : 3 * nh]
        gain = jnp.sum(jnp.where(hi_hot, picked, 0.0), axis=0, keepdims=True)
        gain = jnp.broadcast_to(gain, (8, 128))
        zero8 = jnp.zeros((8, 128), F32)
        parts = jnp.concatenate([*split3(gain), zero8], axis=0).astype(BF16)
        for c in range(CHUNKS):
            wide = dot(parts, gt[:, span(c)])
            pg[:, span(c)] = wide[0:8] + wide[8:16] + wide[16:24]
        st[...] = jnp.zeros_like(st)

    def tv_piece(i):
        for c in range(CHUNKS):
            pl.when(low_ok)(lambda: halo_copy(0, i * CHUNKS + c).wait_recv())
            pl.when(high_ok)(lambda: halo_copy(1, i * CHUNKS + c).wait_recv())
        for c in range(CHUNKS):
            left = 0 if c == 0 else 128
            right = 0 if c == CHUNKS - 1 else 128
            begin = c * width - left
            full = width + left + right
            lane = lax.broadcasted_iota(jnp.int32, (prow, full), 1)

            def plane(z):
                if z < 0:
                    return halo[0, i * prow : (i + 1) * prow, begin : begin + full]
                if z == planes:
                    return halo[1, i * prow : (i + 1) * prow, begin : begin + full]
                r = z * xd + i * prow
                return vol[r : r + prow, begin : begin + full]

            here = plane(-1)
            before = None
            for z in range(-1, planes):
                above = plane(z + 1)
                dz = above - here
                shifted = pltpu.roll(here, full - 1, 1)
                if right == 0:
                    shifted = jnp.where(lane == full - 1, 0.0, shifted)
                du = shifted - here
                inv = lax.rsqrt(dz * dz + du * du + 0.25)
                fz = dz * inv
                if z >= 0:
                    fu = du * inv
                    moved = pltpu.roll(fu, 1, 1)
                    if left == 0:
                        moved = jnp.where(lane == 0, 0.0, moved)
                    smooth = before - fz + moved - fu
                    r = z * xd + i * prow
                    new = here - 0.2 * smooth
                    base[r : r + prow, c * width : (c + 1) * width] = new[:, left : left + width]
                before = fz
                here = above

    sub = min(256, width)

    def tiles(c, body):
        @pl.loop(0, width // sub)
        def _(t):
            body(pl.ds(pl.multiple_of(c * width + t * sub, sub), sub))

    wrows = w.shape[0]
    half = groups * lr

    def stage0(c):
        vol_copies[c].wait()

        def body(u):
            vhi, vlo = split2(vol[:, u])
            first = dot(wst[...], vhi)
            lines = first[:wrows] + first[wrows:] + dot(wst[0:wrows, :], vlo)
            part[0, :, u] = lines[:half]
            part[1, :, u] = lines[half:]

        tiles(c, body)
        start(A, c)

    def stage1(c):
        arrive(A, c)
        u = span(c)
        total = part[core, :, u] + ra[:, u]
        for g in range(groups):
            acc[g, :, u] = total[g * lr : (g + 1) * lr]
        start(B, c)

    def stage2(c):
        arrive(B, c)
        u = span(c)
        lin[2, :, u] = acc[y, :, u] + rb[:, u]
        start(FQ, c)
        start(FP, c)
        start(FM, c)

    def stage3(c):
        arrive(FQ, c)
        start(FR, c)

    brows = taps * lr

    def stage4(c):
        arrive(FP, c)
        arrive(FM, c)
        arrive(FR, c)
        meas_copies[c].wait()

        def body(u):
            lhi, llo = split2(lin[:, :, u].reshape(brows, sub))
            parts = [lhi, llo, lhi]
            if bt.shape[1] > 3 * brows:
                parts.append(jnp.zeros((bt.shape[1] - 3 * brows, sub), BF16))
            proj = dot(bt[...], jnp.concatenate(parts, axis=0))
            gain = pg[0:1, u]
            residual = gain * proj - meas[:, u]
            weighted = gain * residual
            st[0:1, u] = jnp.sum(residual * proj, axis=0, keepdims=True)
            st[1:2, u] = jnp.sum(proj * proj, axis=0, keepdims=True)
            hi, lo = split2(weighted)
            first = dot(bst[...], hi)
            terms = first[:brows] + first[brows:] + dot(bst[0:brows, :], lo)
            cb[:, :, u] = terms.reshape(taps, lr, sub)

        tiles(c, body)
        start(BD, c)
        start(BS, c)

    def stage5(c):
        arrive(BD, c)
        u = span(c)
        pb[:, u] = cb[3 - 2 * par, :, u] + rd[1 - par, :, u]
        start(BP, c)

    def stage6(c):
        arrive(BS, c)
        arrive(BP, c)
        u = span(c)
        img[core, y, :, u] = cb[2, :, u] + rd[par, :, u] + rs[:, u] + rp[:, u]
        start(GY, c)

    def gather_in(c):
        u = span(c)
        pltpu.make_async_remote_copy(
            src_ref=img.at[core, y, :, u], dst_ref=img.at[core, 1 - y, :, u],
            send_sem=send_sem.at[GY, c], recv_sem=recv_sem.at[GY, c],
            device_id=(s, (1 - y) * 2 + core), device_id_type=MESH,
        ).wait_recv()

    def stage7(c):
        gather_in(c)
        start(GC, c)

    def stage8(c):
        u = span(c)
        pltpu.make_async_remote_copy(
            src_ref=img.at[core, :, :, u], dst_ref=img.at[1 - core, :, :, u],
            send_sem=send_sem.at[GC, c], recv_sem=recv_sem.at[GC, c],
            device_id=(s, other), device_id_type=MESH,
        ).wait_recv()

        def body(u):
            ihi, ilo = split2(img[:, :, :, u].reshape(wrows, sub))
            parts = [ihi, ilo, ihi]
            if wt.shape[1] > 3 * wrows:
                parts.append(jnp.zeros((wt.shape[1] - 3 * wrows, sub), BF16))
            gradient = dot(wt[...], jnp.concatenate(parts, axis=0))
            outv[:, u] = base[:, u] - 0.2 * gradient

        tiles(c, body)

    def gain_peer(i):
        return pltpu.make_async_remote_copy(
            src_ref=ga, dst_ref=gr.at[i - 1], send_sem=ks_sem.at[i - 1], recv_sem=kr_sem.at[i - 1],
            device_id=(s, lax.rem(ang + i, na)), device_id_type=MESH,
        )

    def gain_first():
        rows = jnp.concatenate([*split3(st[...]), jnp.zeros(st.shape, F32)], axis=0).astype(BF16)
        sums = dot_nt(rows, gt[...])
        sums = sums[0:8] + sums[8:16] + sums[16:24]
        lane_row = lax.broadcasted_iota(jnp.int32, (8, 128), 0)
        ga[...] = jnp.where(lane_row < 2, sums, gm[...])
        for i in range(1, na):
            gain_peer(i).start()

    def gain_slab(i, slot):
        return pltpu.make_async_remote_copy(
            src_ref=gs.at[slot], dst_ref=gs.at[slot], send_sem=ss_sem.at[i], recv_sem=sr_sem.at[slot],
            device_id=(lax.rem(s + i, n), ang), device_id_type=MESH,
        )

    def gain_second():
        total = ga[...]
        for i in range(1, na):
            gain_peer(i).wait_recv()
            total = total + gr[i - 1]
        lane_row = lax.broadcasted_iota(jnp.int32, (8, 128), 0)
        gs[s] = jnp.where(lane_row < 2, total, gm[...])

        @pl.loop(1, n)
        def _(i):
            gain_slab(i, s).start()

    def gain_last():
        @pl.loop(1, n)
        def _(i):
            gain_slab(i, lax.rem(s + i, n)).wait_recv()

        nh = gv.shape[0]

        def body(i, total):
            m = gs[i]
            lo_hot = jnp.where(
                lax.broadcasted_iota(jnp.int32, (128, 128), 0).astype(F32) == m[3:4], 1.0, 0.0
            ).astype(BF16)
            hi_hot = lax.broadcasted_iota(jnp.int32, (nh, 128), 0).astype(F32) == m[2:3]
            rows = [
                jnp.where(hi_hot, x, 0.0) for k in range(2) for x in split3(m[k : k + 1])
            ]
            return total + dot_nt(jnp.concatenate(rows, axis=0).astype(BF16), lo_hot)

        total = lax.fori_loop(0, n, body, jnp.zeros((6 * nh, 128), F32))
        cross = total[:nh] + total[nh : 2 * nh] + total[2 * nh : 3 * nh]
        energy = total[3 * nh : 4 * nh] + total[4 * nh : 5 * nh] + total[5 * nh :]
        gain_out[...] = gv[...] - cross / (energy + 1.0)

    stages = (stage0, stage1, stage2, stage3, stage4, stage5, stage6, stage7, stage8)
    events = []
    for c in range(CHUNKS):
        for k, stage in enumerate(stages):
            events.append((LAGS[k] + c * PERIODS[k], functools.partial(stage, c)))
    last = HALO_FROM
    for i in range(pieces):
        last = HALO_FROM if i < HALO_EARLY else HALO_NEXT + (i - HALO_EARLY) * HALO_EVERY
        events.append((last, functools.partial(halo_start, i)))
        if i % CHUNKS == CHUNKS - 1:
            loaded = LAGS[0] + (CHUNKS - 1) * PERIODS[0]
            ready = max(min(last + TV_AFTER, LAGS[8] - 0.1), last + 0.01, loaded + 0.01)
            events.append((ready, functools.partial(tv_piece, i // CHUNKS)))
    events.append((PREP_AT[0], prepare))
    events.append((PREP_AT[1], prepare_gain))
    forward_end = LAGS[4] + (CHUNKS - 1) * PERIODS[4]
    for after, run in zip(GAIN_AFTER, (gain_first, gain_second, gain_last)):
        events.append((forward_end + after, run))
    for _, run in sorted(events, key=lambda e: e[0]):
        run()

    for c in range(CHUNKS):
        for kind in range(KINDS):
            guarded(sends, kind, lambda: make(kind, c).wait_send())
    for i in range(pieces):
        pl.when(high_ok)(lambda: halo_copy(0, i).wait_send())
        pl.when(low_ok)(lambda: halo_copy(1, i).wait_send())
    for i in range(1, na):
        gain_peer(i).wait_send()

    @pl.loop(1, n)
    def _(i):
        gain_slab(i, s).wait_send()


def local(n, na, volume, measured, incidence, row_weights, path_table, subset, gain_map, gain_values):
    planes, xd, cols = volume.shape
    al, block, _ = measured.shape
    taps = row_weights.shape[1]
    params = gain_values.shape[0]
    groups = na // 2
    assert taps == 5 and n % 2 == 0 and na == 4 and params % 128 == 0 and cols // block <= 128
    lr = al * planes
    kv = planes * xd
    wrows = na * lr
    brows = taps * lr
    pieces = ROW_PIECES * CHUNKS
    up = lambda v: -(-v // 128) * 128
    vm = pltpu.VMEM
    dma = pltpu.SemaphoreType.DMA
    scratch = [
        vm((kv, cols), F32), vm((al * block, cols), F32), vm((kv, cols), F32),
        vm((2, xd, cols), F32),
        vm((wrows, kv), F32), vm((2 * wrows, kv), BF16), vm((kv, up(3 * wrows)), BF16),
        vm((brows, al * block), F32), vm((2 * brows, al * block), BF16),
        vm((al * block, up(3 * brows)), BF16),
        vm((2, groups * lr, cols), F32), vm((groups * lr, cols), F32), vm((groups, lr, cols), F32),
        vm((lr, cols), F32),
        vm((taps, lr, cols), F32), vm((taps, lr, cols), F32), vm((2, lr, cols), F32),
        vm((lr, cols), F32), vm((lr, cols), F32), vm((lr, cols), F32),
        vm((2, groups, lr, cols), F32),
        vm((128, cols), BF16), vm((8, cols), F32), vm((8, cols), F32),
        vm((8, 128), F32), vm((8, 128), F32), vm((na - 1, 8, 128), F32), vm((n, 8, 128), F32),
        vm((subset.shape[0], path_table.shape[0]), F32),
        dma((CHUNKS,)), dma((CHUNKS,)), dma((KINDS, CHUNKS)), dma((KINDS, CHUNKS)),
        dma((2, pieces)), dma((2, pieces)), dma((na - 1,)), dma((na - 1,)), dma((n,)), dma((n,)),
    ]
    smem = pl.BlockSpec(memory_space=pltpu.SMEM)
    vmem = pl.BlockSpec(memory_space=pltpu.VMEM)
    hbm = pl.BlockSpec(memory_space=pl.ANY)
    out, gain = pl.pallas_call(
        functools.partial(kernel, n, na, planes, xd, al, block),
        out_shape=(
            pltpu.VMEM((kv, cols), F32),
            pltpu.VMEM((params // 128, 128), F32),
        ),
        in_specs=[smem, smem, hbm, hbm, vmem, vmem, vmem, vmem],
        out_specs=(vmem, vmem),
        scratch_shapes=scratch,
        compiler_params=pltpu.CompilerParams(
            collective_id=0, has_side_effects=True, vmem_limit_bytes=56 * 1024 * 1024
        ),
        name="step",
    )(
        incidence, subset, volume.reshape(kv, cols), measured.reshape(al * block, cols),
        row_weights, path_table.T, gain_map, gain_values.reshape(params // 128, 128),
    )
    return out.reshape(planes, xd, cols), gain.reshape(params)


def solution(mesh):
    in_specs = (
        P("slab", "ang", None),
        P("ang", "slab", None),
        P("ang", "slab", None),
        P("ang", None, None, None),
        P(None, "ang"),
        P(),
        P("slab", None),
        P(),
    )
    out_specs = (P("slab", "ang", None), P())
    body = functools.partial(local, mesh.shape["slab"], mesh.shape["ang"])
    return jax.shard_map(body, mesh=mesh, in_specs=in_specs, out_specs=out_specs, check_vma=False)
```
